256 devices in a mesh: dp: 8 (over y, core), ctx: 32 (over x, z).
Axes of the slice: x: 4, y: 4, z: 8, core: 2. Of those that a mesh axis runs over, the one named last changes fastest.
Arguments:
- query_rows: bfloat16 [8, 16384, 1024], P('dp', 'ctx'), may hold values from -6 to 6
- key_rows: bfloat16 [8, 16384, 1024], P('dp', 'ctx'), may hold values from -6 to 6
- value_rows: bfloat16 [8, 16384, 1024], P('dp', 'ctx'), may hold values from -6 to 6
- query_gain: float32 [128], replicated, may hold values from 0.5 to 1.5
- key_gain: float32 [128], replicated, may hold values from 0.5 to 1.5
- selected: int32 [8, 32, 3], P('dp', 'ctx'), may hold values from 0 to 30, as said below
- output_grad: bfloat16 [8, 16384, 1024], P('dp', 'ctx'), may hold values from -6 to 6
Outputs:
- attended: bfloat16 [8, 16384, 1024], P('dp', 'ctx')
- query_grad: bfloat16 [8, 16384, 1024], P('dp', 'ctx')
- key_grad: bfloat16 [8, 16384, 1024], P('dp', 'ctx')
- value_grad: bfloat16 [8, 16384, 1024], P('dp', 'ctx')
- query_gain_grad: float32 [128], replicated
- key_gain_grad: float32 [128], replicated
The draws below stay inside these ranges and needn't reach their ends.
Inputs may be any that keep to these rules, and one draw needn't show every extreme that they name: selected[b, i, 0] is 0 for every query block i, and selected[b, i, 2] is i - 1 for every i >= 2. Every entry of row i lies in 0 to i, and an entry equal to i names no block. Entries below i are distinct within a row. For i >= 3 every entry is below i.
All inputs are finite; a program needn't handle non-finite values.
Results may differ from the reference program's by a relative error of at most 0.012.
Values may be sent and summed in bfloat16 or wider, within the bound.
A program may use at most 128 MiB of HBM per device.

```python
import jax
import jax.numpy as jnp
from jax import lax

HEADS = 8
HEAD_DIM = 128
ATT_WIDTH = 1024
BLOCK = 512
TOPK = 3
NUM_BLOCKS = 32
LENGTH = 16384
BATCH = 8


def draw_selected(key, part):
    priority = jax.random.randint(jax.random.fold_in(key, 11), (BATCH, NUM_BLOCKS, NUM_BLOCKS), 0, 3 * NUM_BLOCKS)
    row_ids = jnp.arange(NUM_BLOCKS)[:, None]
    column_ids = jnp.arange(NUM_BLOCKS)[None, :]
    allowed = (column_ids >= 1) & (column_ids < row_ids - 1)
    ranked = jnp.where(allowed, (priority - column_ids) * NUM_BLOCKS + (NUM_BLOCKS - 1 - column_ids), -8 * NUM_BLOCKS * NUM_BLOCKS - column_ids)
    _, picked = lax.top_k(ranked, TOPK - 2)
    picked_ok = jnp.take_along_axis(jnp.broadcast_to(allowed, ranked.shape), picked, axis=-1)
    middle = jnp.where(picked_ok, picked, jnp.broadcast_to(row_ids[None], picked.shape))
    previous = jnp.where(row_ids >= 2, row_ids - 1, row_ids)
    trailing = jnp.broadcast_to(previous[None], (BATCH, NUM_BLOCKS, 1))
    leading = jnp.zeros((BATCH, NUM_BLOCKS, 1), jnp.int32)
    return jnp.concatenate([leading, middle.astype(jnp.int32), trailing.astype(jnp.int32)], axis=-1)


def block_scale(rng, extent, cuts, least, largest):
    loudness, own = 1.0, jax.random.fold_in(rng, 6)
    for axis_at, shards_of in cuts:
        draws = jnp.exp(jax.random.uniform(jax.random.fold_in(own, axis_at), (shards_of,), jnp.float32, least / len(cuts), largest / len(cuts)))
        loudness = loudness * jnp.repeat(draws, extent[axis_at] // shards_of).reshape([-1 if axis == axis_at else 1 for axis in range(len(extent))])
    return loudness


def bell_draw(own_key, extent, deviation, reach, cuts=(), held_as=jnp.bfloat16):
    drawn = jax.random.normal(own_key, extent, jnp.float32) * deviation
    if len(cuts) > 0:
        drawn = block_scale(own_key, extent, cuts, -0.22, 0.18) * drawn
    return jnp.clip(drawn, min=-reach, max=reach).astype(held_as)


def setup_inputs(seed: int = 0) -> dict:
    arg_keys = jax.random.split(jax.random.key(seed), 8)
    query_rows = bell_draw(arg_keys[0], (BATCH, LENGTH, ATT_WIDTH), 1.0, 6.0, ((0, 8), (1, 32)))
    key_rows = bell_draw(arg_keys[1], (BATCH, LENGTH, ATT_WIDTH), 1.0, 6.0, ((0, 8), (1, 32)))
    value_rows = bell_draw(arg_keys[2], (BATCH, LENGTH, ATT_WIDTH), 1.0, 6.0, ((0, 8), (1, 32)))
    query_gain = jnp.clip(1.0 + 0.1 * jax.random.normal(arg_keys[3], (HEAD_DIM,), jnp.float32), 0.5, 1.5)
    key_gain = jnp.clip(1.0 + 0.1 * jax.random.normal(arg_keys[4], (HEAD_DIM,), jnp.float32), 0.5, 1.5)
    selected = draw_selected(jax.random.fold_in(arg_keys[7], 71), 0)
    output_grad = bell_draw(arg_keys[6], (BATCH, LENGTH, ATT_WIDTH), 1.0, 6.0, ((0, 8), (1, 32)))
    return {"query_rows": query_rows, "key_rows": key_rows, "value_rows": value_rows, "query_gain": query_gain, "key_gain": key_gain, "selected": selected, "output_grad": output_grad}


def head_norm(inputs, gain_vector):
    head_dim = gain_vector.shape[0]
    shaped = inputs.reshape(inputs.shape[:-1] + (inputs.shape[-1] // head_dim, head_dim))
    factor = lax.rsqrt(lax.optimization_barrier(jnp.mean(shaped * shaped, axis=-1, keepdims=True)) + 1e-06)
    return (shaped * factor * gain_vector).reshape(inputs.shape)

def rounded(block_array):
    return lax.optimization_barrier(block_array.astype(jnp.bfloat16)).astype(jnp.float32)

def product(pattern, left, right):
    return jnp.einsum(pattern, left, right, precision=lax.Precision.HIGHEST)

def block_pass(query_block, key_list, value_list, visible_list, grad_block):
    score_scale = HEAD_DIM ** (-0.5)
    weight_list = []
    row_total = 0.0
    for key_block, visible in zip(key_list, visible_list):
        weights = jnp.exp(score_scale * product('qhd,khd->hqk', query_block, key_block)) * visible
        row_total = row_total + lax.optimization_barrier(jnp.sum(weights, axis=-1))
        weight_list.append(weights)
    prob_list = [rounded(weights / row_total[:, :, None]) for weights in weight_list]
    accumulated = 0.0
    for prob_block, value_block in zip(prob_list, value_list):
        accumulated = accumulated + product('hqk,khd->qhd', prob_block, value_block)
    output = rounded(accumulated)
    row_delta = product('qhd,qhd->hq', grad_block, output)
    query_grad = 0.0
    key_terms = []
    value_terms = []
    for prob_block, key_block, value_block in zip(prob_list, key_list, value_list):
        grad_probs = product('qhd,khd->hqk', grad_block, value_block)
        grad_scores = rounded(prob_block * (grad_probs - row_delta[:, :, None]))
        value_terms.append(product('hqk,qhd->khd', prob_block, grad_block))
        key_terms.append(score_scale * product('hqk,qhd->khd', grad_scores, query_block))
        query_grad = query_grad + score_scale * product('hqk,khd->qhd', grad_scores, key_block)
    return (output, query_grad, key_terms, value_terms)

def reference(query_rows, key_rows, value_rows, query_gain, key_gain, selected, output_grad):
    query_float = query_rows.astype(jnp.float32)
    key_float = key_rows.astype(jnp.float32)
    query_normed = head_norm(query_float, query_gain).astype(jnp.bfloat16)
    key_normed = head_norm(key_float, key_gain).astype(jnp.bfloat16)
    positions = jnp.arange(BLOCK)
    causal = (positions[None, :] <= positions[:, None]).astype(jnp.float32)[None]
    block_shape = (NUM_BLOCKS, BLOCK, HEADS, HEAD_DIM)

    def one_sequence(packed):
        query_seq, key_seq, value_seq, chosen, grad_seq = packed
        query_blocks = query_seq.astype(jnp.float32).reshape(block_shape)
        key_blocks = key_seq.astype(jnp.float32).reshape(block_shape)
        value_blocks = value_seq.astype(jnp.float32).reshape(block_shape)
        grad_blocks = grad_seq.astype(jnp.float32).reshape(block_shape)

        def one_block(block_index):
            key_list = [key_blocks[block_index]]
            value_list = [value_blocks[block_index]]
            visible_list = [causal]
            for slot_index in range(TOPK):
                target = chosen[block_index, slot_index]
                key_list.append(key_blocks[target])
                value_list.append(value_blocks[target])
                visible_list.append((target != block_index).astype(jnp.float32))
            output, query_grad, key_terms, value_terms = block_pass(query_blocks[block_index], key_list, value_list, visible_list, grad_blocks[block_index])
            remote_keys = jnp.stack([grad_term.astype(jnp.bfloat16) for grad_term in key_terms[1:]])
            remote_values = jnp.stack([grad_term.astype(jnp.bfloat16) for grad_term in value_terms[1:]])
            return (output.astype(jnp.bfloat16), query_grad, key_terms[0], value_terms[0], remote_keys, remote_values)
        outputs, query_grads, own_keys, own_values, remote_keys, remote_values = lax.map(one_block, jnp.arange(NUM_BLOCKS))
        targets = chosen.reshape(-1).astype(jnp.int32)
        flat_count = NUM_BLOCKS * TOPK
        key_sums = rounded(jax.ops.segment_sum(remote_keys.astype(jnp.float32).reshape(flat_count, -1), targets, num_segments=NUM_BLOCKS))
        value_sums = rounded(jax.ops.segment_sum(remote_values.astype(jnp.float32).reshape(flat_count, -1), targets, num_segments=NUM_BLOCKS))
        key_total = own_keys.reshape(NUM_BLOCKS, -1) + key_sums
        value_grad = (own_values.reshape(NUM_BLOCKS, -1) + value_sums).astype(jnp.bfloat16)
        return (outputs.reshape(LENGTH, -1), query_grads.reshape(LENGTH, -1), key_total.reshape(LENGTH, -1), value_grad.reshape(LENGTH, -1))
    attended, query_total, key_total, value_grad = lax.map(one_sequence, (query_normed, key_normed, value_rows, selected, output_grad))
    _, query_pull = jax.vjp(head_norm, query_float, query_gain)
    query_grad, query_gain_grad = query_pull(query_total)
    _, key_pull = jax.vjp(head_norm, key_float, key_gain)
    key_grad, key_gain_grad = key_pull(key_total)
    return (attended, query_grad.astype(jnp.bfloat16), key_grad.astype(jnp.bfloat16), value_grad, query_gain_grad, key_gain_grad)
```

```python
import functools

import jax
import jax.numpy as jnp
from jax import lax
from jax.experimental import pallas as pl
from jax.experimental.pallas import tpu as pltpu
from jax.sharding import PartitionSpec as P

CHUNKS = 2
EPS = 1e-06
OWN, PREV, FIRST, MID = 0, 1, 2, 3
F32, BF16 = jnp.float32, jnp.bfloat16


def dot(left, right, dims):
    return lax.dot_general(left, right, (dims, ((), ())), preferred_element_type=F32)


def body(
    cfg,
    q_ref, k_ref, v_ref, qg_ref, kg_ref, sel_ref, do_ref,
    att_ref, dq_ref, dk_ref, dv_ref, gain_ref,
    kv, hold, pick, fetch, prev, first, w_scr,
    term, own_grad, back, part, sums, coll, prev_back, rx, rz_out, rz,
    sel_tile, table, table_s, links, gq, gk, gbuf, gbuf2,
    send_sem, recv_sem, sel_sem, local_sem, gain_sem,
):
    n, nx, nz, n_dp, chunks, heads, hd, block = (
        cfg[k] for k in ("n", "nx", "nz", "n_dp", "chunks", "heads", "hd", "block")
    )
    rows = block // n
    width = heads * hd // chunks
    per_chunk = heads // chunks
    scale = hd ** (-0.5)
    me = lax.axis_index("ctx")
    my_dp = lax.axis_index("dp")
    x, z = lax.div(me, nz), lax.rem(me, nz)
    up, down = lax.rem(me + 1, n), lax.rem(me + n - 1, n)

    def peer_of(kx, kz):
        return lax.rem(x + kx, nx) * nz + lax.rem(z + kz, nz)

    def each_peer(fn):
        def step(k, carry):
            fn(peer_of(lax.div(k, nz), lax.rem(k, nz)))
            return carry

        lax.fori_loop(1, n, step, 0)

    def each_z(fn):
        def step(k, carry):
            fn(peer_of(0, k), lax.rem(z + k, nz))
            return carry

        lax.fori_loop(1, nz, step, 0)

    def each_x(fn):
        for k in range(1, nx):
            fn(peer_of(k, 0), lax.rem(x + k, nx))

    def remote(src, dst, stage, c, peer):
        return pltpu.make_async_remote_copy(
            src_ref=src,
            dst_ref=dst,
            send_sem=send_sem.at[stage, c],
            recv_sem=recv_sem.at[stage, c],
            device_id={"ctx": peer},
            device_id_type=pl.DeviceIdType.MESH,
        )

    waits = []

    def landed(like, stage, c):
        remote(like, like, stage, c, up).wait_recv()
        waits.append((like, stage, c))

    HOLD, FETCH, BACK, COLL, PREV_F, PREV_B, AG_Z, AG_X, RS_X, RS_Z = range(10)

    barrier = pltpu.get_barrier_semaphore()

    def greet(peer):
        pl.semaphore_signal(
            barrier, inc=1, device_id={"ctx": peer}, device_id_type=pl.DeviceIdType.MESH
        )

    each_peer(greet)
    for k in range(1, n_dp):
        pl.semaphore_signal(
            barrier,
            inc=1,
            device_id={"dp": lax.rem(my_dp + k, n_dp)},
            device_id_type=pl.DeviceIdType.MESH,
        )

    def norm_chunk(c):
        def step(hh, carry):
            at = pl.ds(pl.multiple_of(hh * hd, hd), hd)
            wide = pl.ds(pl.multiple_of(c * width + hh * hd, hd), hd)
            xk = k_ref[0, :, wide].astype(F32)
            factor = lax.rsqrt(jnp.mean(xk * xk, axis=-1, keepdims=True) + EPS)
            kn = (xk * factor * kg_ref[...]).astype(BF16)
            kv[c, :, 0:rows, at] = kn.reshape(n, rows, hd)
            kv[c, :, rows : 2 * rows, at] = v_ref[0, :, wide].reshape(n, rows, hd)
            return carry

        lax.fori_loop(0, per_chunk, step, 0)

    norm_chunk(0)
    sel_tile[...] = jnp.full(sel_tile.shape, sel_ref[0, 0, 1], jnp.int32)
    pl.semaphore_wait(barrier, n - 1 + n_dp - 1)

    def send_table(peer):
        pltpu.make_async_remote_copy(
            src_ref=sel_tile,
            dst_ref=table.at[me],
            send_sem=sel_sem.at[0],
            recv_sem=sel_sem.at[1],
            device_id={"ctx": peer},
            device_id_type=pl.DeviceIdType.MESH,
        ).start()

    each_peer(send_table)
    table[me] = sel_tile[...]

    def send_hold(c):
        each_peer(lambda p: remote(kv.at[c, p], hold[c].at[me], HOLD, c, p).start())
        hold[c][me] = kv[c, me]

    def send_prev(c):
        remote(kv.at[c], prev.at[c], PREV_F, c, up).start()

    send_hold(0)
    for c in range(1, chunks):
        norm_chunk(c)
        send_hold(c)
    for c in range(chunks):
        send_prev(c)

    some = pltpu.make_async_remote_copy(
        src_ref=table.at[pl.ds(0, n - 1)],
        dst_ref=table.at[pl.ds(0, n - 1)],
        send_sem=sel_sem.at[0],
        recv_sem=sel_sem.at[1],
        device_id={"ctx": up},
        device_id_type=pl.DeviceIdType.MESH,
    )
    some.wait_recv()
    to_scalars = pltpu.make_async_copy(table, table_s, local_sem)
    to_scalars.start()
    to_scalars.wait()

    def link(i, carry):
        mine = table_s[i, 0, 0]

        def look(o, found):
            before, last = found
            other = table_s[o, 0, 0]
            before = jnp.where((o < i) & (other == mine), o, before)
            last = jnp.where(other == i, o, last)
            return before, last

        before, last = lax.fori_loop(0, n, look, (jnp.int32(n), jnp.int32(n)))
        links[0, i] = before
        links[1, i] = last
        return carry

    lax.fori_loop(0, n, link, 0)

    def serve(c):
        landed(hold[c].at[pl.ds(0, n - 1)], HOLD, c)
        first[c, me] = hold[c][0]
        each_z(lambda p, _: remote(first.at[c, me], first.at[c, me], AG_Z, c, p).start())

        def send(p):
            pick[c, p] = hold[c][table_s[p, 0, 0]]
            remote(pick.at[c, p], fetch.at[c, me], FETCH, c, p).start()

        each_peer(send)
        fetch[c, me] = hold[c][table_s[me, 0, 0]]

    def spread(c):
        landed(first.at[c, pl.ds(0, nz - 1)], AG_Z, c)
        row = pl.ds(x * nz, nz)
        each_x(lambda p, _: remote(first.at[c, row], first.at[c, row], AG_X, c, p).start())

    for c in range(chunks):
        serve(c)
        spread(c)

    see_prev = (me >= 2).astype(F32)
    see_first = (me >= 1).astype(F32)
    see_mid = jnp.where(table_s[me, 0, 0] != me, 1.0, 0.0).astype(F32)
    see = (None, see_prev, see_first, see_mid)
    stores = (kv, prev, first, fetch)

    def seen(value, b):
        return value if see[b] is None else value * see[b]

    gq[...] = jnp.zeros_like(gq)
    gk[...] = jnp.zeros_like(gk)

    def attend(c):
        def step(hh, carry):
            at = pl.ds(pl.multiple_of(hh * hd, hd), hd)
            wide = pl.ds(pl.multiple_of(c * width + hh * hd, hd), hd)
            xt = q_ref[0, :, wide].astype(F32).T
            factor = lax.rsqrt(jnp.mean(xt * xt, axis=0, keepdims=True) + EPS)
            gain = qg_ref[...]
            qn = (xt * factor * gain).astype(BF16)
            do = do_ref[0, :, wide].astype(F32).T
            do_b = do.astype(BF16)

            def keys(b):
                return stores[b][c, :, 0:rows, at].reshape(block, hd)

            def values(b):
                return stores[b][c, :, rows : 2 * rows, at].reshape(block, hd)

            total = jnp.zeros((1, block), F32)
            acc = jnp.zeros((hd, block), F32)
            for b in (OWN, PREV, FIRST, MID):
                s = dot(keys(b), qn, ((1,), (0,)))
                w = jnp.exp2(s * (scale * 1.4426950408889634))
                if b == OWN:
                    ki = lax.broadcasted_iota(jnp.int32, (block, block), 0)
                    qi = lax.broadcasted_iota(jnp.int32, (block, block), 1)
                    w = jnp.where(ki <= qi, w, 0.0)
                total = total + seen(jnp.sum(w, axis=0, keepdims=True), b)
                wb = w.astype(BF16)
                w_scr[b] = wb
                acc = acc + seen(dot(values(b), wb, ((0,), (0,))), b)
            inv = 1.0 / total
            out = (acc * inv).astype(BF16).astype(F32)
            att_ref[0, :, wide] = out.T.astype(BF16)
            delta = jnp.sum(do * out, axis=0, keepdims=True)
            inv_s = inv * scale
            qs = (qn.astype(F32) * inv_s).astype(BF16)
            dos = (do * inv).astype(BF16)
            dq = jnp.zeros((hd, block), F32)
            for b in (MID, FIRST, PREV, OWN):
                wb = w_scr[b]
                dp = dot(values(b), do_b, ((1,), (0,)))
                ds = (wb.astype(F32) * (dp - delta)).astype(BF16)
                dq = dq + seen(dot(keys(b), ds, ((0,), (0,))), b)
                dk = seen(dot(ds, qs, ((1,), (1,))), b)
                dv = seen(dot(wb, dos, ((1,), (1,))), b)
                if b == OWN:
                    own_grad[0, :, wide] = dk
                    own_grad[1, :, wide] = dv
                else:
                    term[b - 1, c, :, 0:rows, at] = dk.astype(BF16).reshape(n, rows, hd)
                    term[b - 1, c, :, rows : 2 * rows, at] = dv.astype(BF16).reshape(n, rows, hd)
            dy = dq * inv_s
            xr = xt * factor
            both = dy * xr
            g = both[:, 0:hd]
            for k in range(1, block // hd):
                g = g + both[:, k * hd : (k + 1) * hd]
            gq[...] += g
            u = dy * gain
            dx = factor * (u - xr * jnp.mean(xr * u, axis=0, keepdims=True))
            dq_ref[0, :, wide] = dx.T.astype(BF16)
            return carry

        lax.fori_loop(0, per_chunk, step, 0)

    def give_back(c):
        mid, head, before = term.at[MID - 1, c], term.at[FIRST - 1, c], term.at[PREV - 1, c]
        each_peer(lambda p: remote(mid.at[p], back.at[c, me], BACK, c, p).start())
        back[c, me] = term[MID - 1, c, me]

        def send_row(p, px):
            remote(head.at[pl.ds(px * nz, nz)], rx.at[c, x], RS_X, c, p).start()

        each_x(send_row)
        rx[c, x] = term[FIRST - 1, c, pl.ds(x * nz, nz)]
        remote(before, prev_back.at[c], PREV_B, c, down).start()

    def fold_first(c):
        landed(rx.at[c, pl.ds(0, nx - 1)], RS_X, c)

        def fold(s, carry):
            total = rx[c, 0, s].astype(F32)
            for k in range(1, nx):
                total = total + rx[c, k, s].astype(F32)
            rz_out[c, s] = total.astype(BF16)
            return carry

        lax.fori_loop(0, nz, fold, 0)
        each_z(lambda p, pz: remote(rz_out.at[c, pz], rz.at[c, z], RS_Z, c, p).start())
        rz[c, z] = rz_out[c, z]

    def collect(c):
        landed(back.at[c, pl.ds(0, n - 1)], BACK, c)
        part[n] = jnp.zeros(part.shape[1:], F32)

        def add(i, carry):
            part[i] = back[c, i].astype(F32) + part[links[0, i]]
            return carry

        lax.fori_loop(0, n, add, 0)

        def settle(j, carry):
            sums[c, j] = part[links[1, j]].astype(BF16)
            return carry

        lax.fori_loop(1, n, settle, 0)
        landed(rz.at[c, pl.ds(0, nz - 1)], RS_Z, c)
        total = part[links[1, 0]]
        for k in range(nz):
            total = total + rz[c, k].astype(F32)
        sums[c, 0] = total.astype(BF16)
        each_peer(lambda p: remote(sums.at[c, p], coll.at[c, me], COLL, c, p).start())
        coll[c, me] = sums[c, me]

    def finish(c):
        landed(prev_back.at[c], PREV_B, c)
        landed(coll.at[c, pl.ds(0, n - 1)], COLL, c)

        def step(hh, carry):
            at = pl.ds(pl.multiple_of(hh * hd, hd), hd)
            wide = pl.ds(pl.multiple_of(c * width + hh * hd, hd), hd)

            def remote_sum(lo):
                one = coll[c, :, lo : lo + rows, at].reshape(block, hd).astype(F32)
                two = prev_back[c, :, lo : lo + rows, at].reshape(block, hd).astype(F32)
                return one + two

            dv_ref[0, :, wide] = (own_grad[1, :, wide] + remote_sum(rows)).astype(BF16)
            dy = own_grad[0, :, wide] + remote_sum(0)
            xk = k_ref[0, :, wide].astype(F32)
            factor = lax.rsqrt(jnp.mean(xk * xk, axis=-1, keepdims=True) + EPS)
            xr = xk * factor
            gk[...] += jnp.sum((dy * xr).reshape(block // 8, 8, hd), axis=0)
            u = dy * kg_ref[...]
            dx = factor * (u - xr * jnp.mean(xr * u, axis=-1, keepdims=True))
            dk_ref[0, :, wide] = dx.astype(BF16)
            return carry

        lax.fori_loop(0, per_chunk, step, 0)

    for c in range(chunks):
        landed(prev.at[c], PREV_F, c)
        landed(fetch.at[c, pl.ds(0, n - 1)], FETCH, c)
        landed(first.at[c, pl.ds(0, (nx - 1) * nz)], AG_X, c)
        attend(c)
        give_back(c)
        if c >= 1:
            fold_first(c - 1)
            collect(c - 1)
    fold_first(chunks - 1)
    collect(chunks - 1)
    for c in range(chunks):
        finish(c)

    q_row = jnp.sum(gq[...].T, axis=0, keepdims=True)
    k_row = jnp.sum(gk[...], axis=0, keepdims=True)
    at = lax.broadcasted_iota(jnp.int32, (8, hd), 0)
    gbuf[me] = jnp.where(at == 0, q_row, jnp.where(at == 1, k_row, 0.0))

    def send_gain(buf, slot, at, where):
        return pltpu.make_async_remote_copy(
            src_ref=buf.at[slot],
            dst_ref=buf.at[slot],
            send_sem=gain_sem.at[at, 0],
            recv_sem=gain_sem.at[at, 1],
            device_id=where,
            device_id_type=pl.DeviceIdType.MESH,
        )

    def all_gain(buf, count, at):
        many = buf.at[pl.ds(0, count - 1)]
        return pltpu.make_async_remote_copy(
            src_ref=many,
            dst_ref=many,
            send_sem=gain_sem.at[at, 0],
            recv_sem=gain_sem.at[at, 1],
            device_id={"ctx": up},
            device_id_type=pl.DeviceIdType.MESH,
        )

    each_peer(lambda p: send_gain(gbuf, me, 0, {"ctx": p}).start())
    all_gain(gbuf, n, 0).wait_recv()
    total = gbuf[0]
    for i in range(1, n):
        total = total + gbuf[i]
    gbuf2[my_dp] = total
    for k in range(1, n_dp):
        send_gain(gbuf2, my_dp, 1, {"dp": lax.rem(my_dp + k, n_dp)}).start()
    all_gain(gbuf2, n_dp, 1).wait_recv()
    total = gbuf2[0]
    for i in range(1, n_dp):
        total = total + gbuf2[i]
    gain_ref[...] = total

    all_gain(gbuf, n, 0).wait_send()
    all_gain(gbuf2, n_dp, 1).wait_send()
    some.wait_send()
    for like, stage, c in waits:
        remote(like, like, stage, c, up).wait_send()


def local(mesh_shape, query_rows, key_rows, value_rows, query_gain, key_gain, selected, output_grad):
    n, n_dp = mesh_shape["ctx"], mesh_shape["dp"]
    nz = 8 if n == 32 else n // 2
    nx = n // nz
    block, model = query_rows.shape[1:]
    hd = query_gain.shape[0]
    heads = model // hd
    chunks = CHUNKS
    cfg = dict(n=n, nx=nx, nz=nz, n_dp=n_dp, chunks=chunks, heads=heads, hd=hd, block=block)
    width, rows = model // chunks, block // n
    slices = (chunks, n, 2 * rows, width)
    vmem = pltpu.VMEM
    row = jax.ShapeDtypeStruct((1, block, model), BF16)
    whole = pl.BlockSpec(memory_space=pltpu.VMEM)
    outs = pl.pallas_call(
        functools.partial(body, cfg),
        out_shape=(row, row, row, row, jax.ShapeDtypeStruct((8, hd), F32)),
        in_specs=[whole] * 5 + [pl.BlockSpec(memory_space=pltpu.SMEM), whole],
        out_specs=(whole,) * 5,
        scratch_shapes=[
            vmem(slices, BF16),
            [vmem(slices[1:], BF16)] * chunks,
            vmem(slices, BF16),
            vmem(slices, BF16),
            vmem(slices, BF16),
            vmem(slices, BF16),
            vmem((4, block, block), BF16),
            vmem((3,) + slices, BF16),
            vmem((2, block, model), F32),
            vmem(slices, BF16),
            vmem((n + 1, 2 * rows, width), F32),
            vmem(slices, BF16),
            vmem(slices, BF16),
            vmem(slices, BF16),
            vmem((chunks, nx, nz, 2 * rows, width), BF16),
            vmem((chunks, nz, 2 * rows, width), BF16),
            vmem((chunks, nz, 2 * rows, width), BF16),
            vmem((8, 128), jnp.int32),
            vmem((n, 8, 128), jnp.int32),
            pltpu.SMEM((n, 8, 128), jnp.int32),
            pltpu.SMEM((2, n), jnp.int32),
            vmem((hd, hd), F32),
            vmem((8, hd), F32),
            vmem((n, 8, hd), F32),
            vmem((n_dp, 8, hd), F32),
            pltpu.SemaphoreType.DMA((10, chunks)),
            pltpu.SemaphoreType.DMA((10, chunks)),
            pltpu.SemaphoreType.DMA((2,)),
            pltpu.SemaphoreType.DMA,
            pltpu.SemaphoreType.DMA((2, 2)),
        ],
        compiler_params=pltpu.CompilerParams(
            collective_id=0, has_side_effects=True, vmem_limit_bytes=60 * 1024 * 1024
        ),
    )(
        query_rows,
        key_rows,
        value_rows,
        query_gain.reshape(hd, 1),
        key_gain.reshape(1, hd),
        selected,
        output_grad,
    )
    attended, query_grad, key_grad, value_grad, gains = outs
    return attended, query_grad, key_grad, value_grad, gains[0], gains[1]


def solution(mesh):
    rows = P("dp", "ctx", None)
    return jax.shard_map(
        functools.partial(local, dict(mesh.shape)),
        mesh=mesh,
        in_specs=(rows, rows, rows, P(), P(), rows, rows),
        out_specs=(rows, rows, rows, rows, P(), P()),
        check_vma=False,
    )
```

```python
import functools

import jax
import jax.numpy as jnp
from jax import lax
from jax.experimental import pallas as pl
from jax.experimental.pallas import tpu as pltpu
from jax.sharding import PartitionSpec as P

CHUNKS = 4
EPS = 1e-06
OWN, PREV, FIRST, MID = 0, 1, 2, 3
F32, BF16 = jnp.float32, jnp.bfloat16


def dot(left, right, dims):
    return lax.dot_general(left, right, (dims, ((), ())), preferred_element_type=F32)


def body(
    cfg,
    q_hbm, k_ref, v_ref, qg_ref, kg_ref, sel_ref, do_hbm,
    att_ref, dq_ref, dk_ref, dv_ref, gain_ref,
    kv, hold, pick, fetch, prev, first, w_scr,
    term, own_grad, back, part, sums, coll, prev_back, rx, rz_out, rz,
    sel_tile, table, links_v, links, gq, gk, gbuf, gbuf2,
    send_sem, recv_sem, sel_sem, local_sem, gain_sem, q_ref, do_ref, in_sem,
):
    n, nx, nz, n_dp, chunks, heads, hd, block = (
        cfg[k] for k in ("n", "nx", "nz", "n_dp", "chunks", "heads", "hd", "block")
    )
    rows = block // n
    width = heads * hd // chunks
    per_chunk = heads // chunks
    scale = hd ** (-0.5)
    me = lax.axis_index("ctx")
    my_dp = lax.axis_index("dp")
    x, z = lax.div(me, nz), lax.rem(me, nz)
    up, down = lax.rem(me + 1, n), lax.rem(me + n - 1, n)

    def peer_of(kx, kz):
        return lax.rem(x + kx, nx) * nz + lax.rem(z + kz, nz)

    def each_peer(fn):
        def step(k, carry):
            fn(peer_of(lax.div(k, nz), lax.rem(k, nz)))
            return carry

        lax.fori_loop(1, n, step, 0)

    def each_z(fn):
        def step(k, carry):
            fn(peer_of(0, k), lax.rem(z + k, nz))
            return carry

        lax.fori_loop(1, nz, step, 0)

    def each_x(fn):
        for k in range(1, nx):
            fn(peer_of(k, 0), lax.rem(x + k, nx))

    def remote(src, dst, stage, c, peer):
        return pltpu.make_async_remote_copy(
            src_ref=src,
            dst_ref=dst,
            send_sem=send_sem.at[stage, c],
            recv_sem=recv_sem.at[stage, c],
            device_id={"ctx": peer},
            device_id_type=pl.DeviceIdType.MESH,
        )

    waits = []

    def landed(like, stage, c):
        remote(like, like, stage, c, up).wait_recv()
        waits.append((like, stage, c))

    HOLD, FETCH, BACK, COLL, PREV_F, PREV_B, AG_Z, AG_X, RS_X, RS_Z = range(10)

    load_q = pltpu.make_async_copy(q_hbm, q_ref, in_sem.at[0])
    load_do = pltpu.make_async_copy(do_hbm, do_ref, in_sem.at[1])
    load_q.start()
    load_do.start()
    barrier = pltpu.get_barrier_semaphore()

    def greet(peer):
        pl.semaphore_signal(
            barrier, inc=1, device_id={"ctx": peer}, device_id_type=pl.DeviceIdType.MESH
        )

    each_peer(greet)
    for k in range(1, n_dp):
        pl.semaphore_signal(
            barrier,
            inc=1,
            device_id={"dp": lax.rem(my_dp + k, n_dp)},
            device_id_type=pl.DeviceIdType.MESH,
        )

    def norm_chunk(c):
        def step(hh, carry):
            at = pl.ds(pl.multiple_of(hh * hd, hd), hd)
            wide = pl.ds(pl.multiple_of(c * width + hh * hd, hd), hd)
            xk = k_ref[0, :, wide].astype(F32)
            factor = lax.rsqrt(jnp.mean(xk * xk, axis=-1, keepdims=True) + EPS)
            kn = (xk * factor * kg_ref[...]).astype(BF16)
            kv[c, :, 0:rows, at] = kn.reshape(n, rows, hd)
            kv[c, :, rows : 2 * rows, at] = v_ref[0, :, wide].reshape(n, rows, hd)
            return carry

        lax.fori_loop(0, per_chunk, step, 0)

    gain_col = jnp.broadcast_to(qg_ref[...], (8, hd)).T[:, 0:1]
    norm_chunk(0)
    sub = lax.broadcasted_iota(jnp.int32, (8, 128), 0)
    lane = lax.broadcasted_iota(jnp.int32, (8, 128), 1)
    sel_tile[...] = jnp.where((sub < 4) | (lane == me), sel_ref[0, 0, 1], 0)
    pl.semaphore_wait(barrier, n - 1 + n_dp - 1)

    def send_table(peer):
        pltpu.make_async_remote_copy(
            src_ref=sel_tile,
            dst_ref=table.at[me],
            send_sem=sel_sem.at[0],
            recv_sem=sel_sem.at[1],
            device_id={"ctx": peer},
            device_id_type=pl.DeviceIdType.MESH,
        ).start()

    each_peer(send_table)
    table[me] = sel_tile[...]

    def send_hold(c):
        each_peer(lambda p: remote(kv.at[c, p], hold[c].at[me], HOLD, c, p).start())
        hold[c][me] = kv[c, me]

    def send_prev(c):
        remote(kv.at[c], prev.at[c], PREV_F, c, up).start()

    send_hold(0)
    for c in range(1, chunks):
        norm_chunk(c)

    some = pltpu.make_async_remote_copy(
        src_ref=table.at[pl.ds(0, n - 1)],
        dst_ref=table.at[pl.ds(0, n - 1)],
        send_sem=sel_sem.at[0],
        recv_sem=sel_sem.at[1],
        device_id={"ctx": up},
        device_id_type=pl.DeviceIdType.MESH,
    )
    some.wait_recv()
    choice = table[:, 0, :]
    spread_out = table[0, 4:8, :]
    for i in range(1, n):
        spread_out = spread_out + table[i, 4:8, :]
    across = jnp.broadcast_to(spread_out[0:1, :], (n, 128))
    row_id = lax.broadcasted_iota(jnp.int32, (n, 128), 0)
    lane_id = lax.broadcasted_iota(jnp.int32, (n, 128), 1)
    before = jnp.where((across == choice) & (lane_id < row_id), lane_id, -1)
    last = jnp.where((across == row_id) & (lane_id < n), lane_id, -1)
    links_v[0] = choice
    for k, found in ((1, before), (2, last)):
        top = jnp.max(found, axis=-1, keepdims=True)
        links_v[k] = jnp.broadcast_to(jnp.where(top < 0, n, top), (n, 128))
    to_scalars = pltpu.make_async_copy(links_v, links, local_sem)
    to_scalars.start()
    to_scalars.wait()

    def link(kind, i):
        return jnp.clip(links[kind, i, 0], 0, n if kind else n - 1)

    def serve(c):
        landed(hold[c].at[pl.ds(0, n - 1)], HOLD, c)
        first[c, me] = hold[c][0]
        each_z(lambda p, _: remote(first.at[c, me], first.at[c, me], AG_Z, c, p).start())

        def send(p):
            pick[c, p] = hold[c][link(0, p)]
            remote(pick.at[c, p], fetch.at[c, me], FETCH, c, p).start()

        each_peer(send)
        fetch[c, me] = hold[c][link(0, me)]

    def spread(c):
        landed(first.at[c, pl.ds(0, nz - 1)], AG_Z, c)
        row = pl.ds(x * nz, nz)
        each_x(lambda p, _: remote(first.at[c, row], first.at[c, row], AG_X, c, p).start())

    def prepare(c):
        serve(c)
        if c + 1 < chunks:
            send_hold(c + 1)
        send_prev(c)
        spread(c)

    prepare(0)
    load_q.wait()
    load_do.wait()

    see_prev = (me >= 2).astype(F32)
    see_first = (me >= 1).astype(F32)
    see_mid = jnp.where(links[0, me, 0] != me, 1.0, 0.0).astype(F32)
    see = (None, see_prev, see_first, see_mid)
    stores = (kv, prev, first, fetch)

    def seen(value, b):
        return value if see[b] is None else value * see[b]

    gq[...] = jnp.zeros_like(gq)
    gk[...] = jnp.zeros_like(gk)

    def attend(c):
        def step(hh, carry):
            at = pl.ds(pl.multiple_of(hh * hd, hd), hd)
            wide = pl.ds(pl.multiple_of(c * width + hh * hd, hd), hd)
            xt = q_ref[0, :, wide].astype(F32).T
            factor = lax.rsqrt(jnp.mean(xt * xt, axis=0, keepdims=True) + EPS)
            gain = gain_col
            qn = (xt * factor * gain).astype(BF16)
            do = do_ref[0, :, wide].astype(F32).T
            do_b = do.astype(BF16)

            def keys(b):
                return stores[b][c, :, 0:rows, at].reshape(block, hd)

            def values(b):
                return stores[b][c, :, rows : 2 * rows, at].reshape(block, hd)

            total = jnp.zeros((1, block), F32)
            acc = jnp.zeros((hd, block), F32)
            for b in (OWN, PREV, FIRST, MID):
                s = dot(keys(b), qn, ((1,), (0,)))
                w = jnp.exp2(s * (scale * 1.4426950408889634))
                if b == OWN:
                    ki = lax.broadcasted_iota(jnp.int32, (block, block), 0)
                    qi = lax.broadcasted_iota(jnp.int32, (block, block), 1)
                    w = jnp.where(ki <= qi, w, 0.0)
                total = total + seen(jnp.sum(w, axis=0, keepdims=True), b)
                wb = w.astype(BF16)
                w_scr[b] = wb
                acc = acc + seen(dot(values(b), wb, ((0,), (0,))), b)
            inv = 1.0 / total
            out = (acc * inv).astype(BF16).astype(F32)
            att_ref[0, :, wide] = out.T.astype(BF16)
            delta = jnp.sum(do * out, axis=0, keepdims=True)
            inv_s = inv * scale
            qs = (qn.astype(F32) * inv_s).astype(BF16)
            dos = (do * inv).astype(BF16)
            dq = jnp.zeros((hd, block), F32)
            for b in (MID, FIRST, PREV, OWN):
                wb = w_scr[b]
                dp = dot(values(b), do_b, ((1,), (0,)))
                ds = (wb.astype(F32) * (dp - delta)).astype(BF16)
                dq = dq + seen(dot(keys(b), ds, ((0,), (0,))), b)
                dk = seen(dot(ds, qs, ((1,), (1,))), b)
                dv = seen(dot(wb, dos, ((1,), (1,))), b)
                if b == OWN:
                    own_grad[0, :, wide] = dk
                    own_grad[1, :, wide] = dv
                else:
                    term[b - 1, c, :, 0:rows, at] = dk.astype(BF16).reshape(n, rows, hd)
                    term[b - 1, c, :, rows : 2 * rows, at] = dv.astype(BF16).reshape(n, rows, hd)
            dy = dq * inv_s
            xr = xt * factor
            both = dy * xr
            g = both[:, 0:hd]
            for k in range(1, block // hd):
                g = g + both[:, k * hd : (k + 1) * hd]
            gq[...] += g
            u = dy * gain
            dx = factor * (u - xr * jnp.mean(xr * u, axis=0, keepdims=True))
            dq_ref[0, :, wide] = dx.T.astype(BF16)
            return carry

        lax.fori_loop(0, per_chunk, step, 0)

    def give_back(c):
        mid, head = term.at[MID - 1, c], term.at[FIRST - 1, c]
        each_peer(lambda p: remote(mid.at[p], back.at[c, me], BACK, c, p).start())
        back[c, me] = term[MID - 1, c, me]

        def send_row(p, px):
            remote(head.at[pl.ds(px * nz, nz)], rx.at[c, x], RS_X, c, p).start()

        each_x(send_row)
        rx[c, x] = term[FIRST - 1, c, pl.ds(x * nz, nz)]
        if c + 1 < chunks:
            send_prev_back(c)

    def send_prev_back(c):
        remote(term.at[PREV - 1, c], prev_back.at[c], PREV_B, c, down).start()

    def fold_first(c):
        landed(rx.at[c, pl.ds(0, nx - 1)], RS_X, c)

        def fold(s, carry):
            total = rx[c, 0, s].astype(F32)
            for k in range(1, nx):
                total = total + rx[c, k, s].astype(F32)
            rz_out[c, s] = total.astype(BF16)
            return carry

        lax.fori_loop(0, nz, fold, 0)
        each_z(lambda p, pz: remote(rz_out.at[c, pz], rz.at[c, z], RS_Z, c, p).start())
        rz[c, z] = rz_out[c, z]

    def collect(c):
        landed(back.at[c, pl.ds(0, n - 1)], BACK, c)
        if c + 1 == chunks:
            send_prev_back(c)
        part[n] = jnp.zeros(part.shape[1:], F32)

        def add(i, carry):
            part[i] = back[c, i].astype(F32) + part[link(1, i)]
            return carry

        lax.fori_loop(0, n, add, 0)

        def settle(j, carry):
            sums[c, j] = part[link(2, j)].astype(BF16)
            return carry

        lax.fori_loop(1, n, settle, 0)
        landed(rz.at[c, pl.ds(0, nz - 1)], RS_Z, c)
        total = part[link(2, 0)]
        for k in range(nz):
            total = total + rz[c, k].astype(F32)
        sums[c, 0] = total.astype(BF16)
        each_peer(lambda p: remote(sums.at[c, p], coll.at[c, me], COLL, c, p).start())
        coll[c, me] = sums[c, me]

    def finish(c):
        landed(prev_back.at[c], PREV_B, c)
        landed(coll.at[c, pl.ds(0, n - 1)], COLL, c)

        def step(hh, carry):
            at = pl.ds(pl.multiple_of(hh * hd, hd), hd)
            wide = pl.ds(pl.multiple_of(c * width + hh * hd, hd), hd)

            def remote_sum(lo):
                one = coll[c, :, lo : lo + rows, at].reshape(block, hd).astype(F32)
                two = prev_back[c, :, lo : lo + rows, at].reshape(block, hd).astype(F32)
                return one + two

            dv_ref[0, :, wide] = (own_grad[1, :, wide] + remote_sum(rows)).astype(BF16)
            dy = own_grad[0, :, wide] + remote_sum(0)
            xk = k_ref[0, :, wide].astype(F32)
            factor = lax.rsqrt(jnp.mean(xk * xk, axis=-1, keepdims=True) + EPS)
            xr = xk * factor
            gk[...] += jnp.sum((dy * xr).reshape(block // 8, 8, hd), axis=0)
            u = dy * kg_ref[...]
            dx = factor * (u - xr * jnp.mean(xr * u, axis=-1, keepdims=True))
            dk_ref[0, :, wide] = dx.astype(BF16)
            return carry

        lax.fori_loop(0, per_chunk, step, 0)

    for c in range(chunks):
        if c + 1 < chunks:
            prepare(c + 1)
        landed(prev.at[c], PREV_F, c)
        landed(fetch.at[c, pl.ds(0, n - 1)], FETCH, c)
        landed(first.at[c, pl.ds(0, (nx - 1) * nz)], AG_X, c)
        attend(c)
        give_back(c)
        if c >= 1:
            fold_first(c - 1)
            collect(c - 1)
    fold_first(chunks - 1)
    collect(chunks - 1)
    for c in range(chunks):
        finish(c)

    q_row = jnp.sum(gq[...].T, axis=0, keepdims=True)
    k_row = jnp.sum(gk[...], axis=0, keepdims=True)
    at = lax.broadcasted_iota(jnp.int32, (8, hd), 0)
    gbuf[me] = jnp.where(at == 0, q_row, jnp.where(at == 1, k_row, 0.0))

    def send_gain(buf, slot, at, where):
        return pltpu.make_async_remote_copy(
            src_ref=buf.at[slot],
            dst_ref=buf.at[slot],
            send_sem=gain_sem.at[at, 0],
            recv_sem=gain_sem.at[at, 1],
            device_id=where,
            device_id_type=pl.DeviceIdType.MESH,
        )

    def all_gain(buf, count, at):
        many = buf.at[pl.ds(0, count - 1)]
        return pltpu.make_async_remote_copy(
            src_ref=many,
            dst_ref=many,
            send_sem=gain_sem.at[at, 0],
            recv_sem=gain_sem.at[at, 1],
            device_id={"ctx": up},
            device_id_type=pl.DeviceIdType.MESH,
        )

    each_peer(lambda p: send_gain(gbuf, me, 0, {"ctx": p}).start())
    all_gain(gbuf, n, 0).wait_recv()
    total = gbuf[0]
    for i in range(1, n):
        total = total + gbuf[i]
    gbuf2[my_dp] = total
    for k in range(1, n_dp):
        send_gain(gbuf2, my_dp, 1, {"dp": lax.rem(my_dp + k, n_dp)}).start()
    all_gain(gbuf2, n_dp, 1).wait_recv()
    total = gbuf2[0]
    for i in range(1, n_dp):
        total = total + gbuf2[i]
    gain_ref[...] = total

    all_gain(gbuf, n, 0).wait_send()
    all_gain(gbuf2, n_dp, 1).wait_send()
    some.wait_send()
    for like, stage, c in waits:
        remote(like, like, stage, c, up).wait_send()


def local(mesh_shape, query_rows, key_rows, value_rows, query_gain, key_gain, selected, output_grad):
    n, n_dp = mesh_shape["ctx"], mesh_shape["dp"]
    nz = 8 if n == 32 else n // 2
    nx = n // nz
    block, model = query_rows.shape[1:]
    hd = query_gain.shape[0]
    heads = model // hd
    chunks = CHUNKS
    cfg = dict(n=n, nx=nx, nz=nz, n_dp=n_dp, chunks=chunks, heads=heads, hd=hd, block=block)
    width, rows = model // chunks, block // n
    slices = (chunks, n, 2 * rows, width)
    vmem = pltpu.VMEM
    row = jax.ShapeDtypeStruct((1, block, model), BF16)
    whole = pl.BlockSpec(memory_space=pltpu.VMEM)
    anywhere = pl.BlockSpec(memory_space=pl.ANY)
    outs = pl.pallas_call(
        functools.partial(body, cfg),
        out_shape=(row, row, row, row, jax.ShapeDtypeStruct((8, hd), F32)),
        in_specs=[anywhere] + [whole] * 4 + [pl.BlockSpec(memory_space=pltpu.SMEM), anywhere],
        out_specs=(whole,) * 5,
        scratch_shapes=[
            vmem(slices, BF16),
            [vmem(slices[1:], BF16)] * chunks,
            vmem(slices, BF16),
            vmem(slices, BF16),
            vmem(slices, BF16),
            vmem(slices, BF16),
            vmem((4, block, block), BF16),
            vmem((3,) + slices, BF16),
            vmem((2, block, model), F32),
            vmem(slices, BF16),
            vmem((n + 1, 2 * rows, width), F32),
            vmem(slices, BF16),
            vmem(slices, BF16),
            vmem(slices, BF16),
            vmem((chunks, nx, nz, 2 * rows, width), BF16),
            vmem((chunks, nz, 2 * rows, width), BF16),
            vmem((chunks, nz, 2 * rows, width), BF16),
            vmem((8, 128), jnp.int32),
            vmem((n, 8, 128), jnp.int32),
            vmem((3, n, 128), jnp.int32),
            pltpu.SMEM((3, n, 128), jnp.int32),
            vmem((hd, hd), F32),
            vmem((8, hd), F32),
            vmem((n, 8, hd), F32),
            vmem((n_dp, 8, hd), F32),
            pltpu.SemaphoreType.DMA((10, chunks)),
            pltpu.SemaphoreType.DMA((10, chunks)),
            pltpu.SemaphoreType.DMA((2,)),
            pltpu.SemaphoreType.DMA,
            pltpu.SemaphoreType.DMA((2, 2)),
            vmem((1, block, model), BF16),
            vmem((1, block, model), BF16),
            pltpu.SemaphoreType.DMA((2,)),
        ],
        compiler_params=pltpu.CompilerParams(
            collective_id=0, has_side_effects=True, vmem_limit_bytes=60 * 1024 * 1024
        ),
    )(
        query_rows,
        key_rows,
        value_rows,
        query_gain.reshape(1, hd),
        key_gain.reshape(1, hd),
        selected,
        output_grad,
    )
    attended, query_grad, key_grad, value_grad, gains = outs
    return attended, query_grad, key_grad, value_grad, gains[0], gains[1]


def solution(mesh):
    rows = P("dp", "ctx", None)
    return jax.shard_map(
        functools.partial(local, dict(mesh.shape)),
        mesh=mesh,
        in_specs=(rows, rows, rows, P(), P(), rows, rows),
        out_specs=(rows, rows, rows, rows, P(), P()),
        check_vma=False,
    )
```

```python
import functools

import jax
import jax.numpy as jnp
from jax import lax
from jax.experimental import pallas as pl
from jax.experimental.pallas import tpu as pltpu
from jax.sharding import PartitionSpec as P

CHUNKS = 4
EPS = 1e-06
OWN, PREV, FIRST, MID = 0, 1, 2, 3
F32, BF16 = jnp.float32, jnp.bfloat16


def dot(left, right, dims):
    return lax.dot_general(left, right, (dims, ((), ())), preferred_element_type=F32)


def body(
    cfg,
    q_hbm, k_ref, v_ref, qg_ref, kg_ref, sel_ref, do_hbm,
    att_ref, dq_ref, dk_ref, dv_ref, q_gain_ref, k_gain_ref,
    kv, hold, pick, fetch, prev, first, w_scr,
    term, own_grad, back, part, sums, coll, prev_back, rx, rz_out, rz,
    sel_tile, table, links_v, links, gq, gk, gbuf, gbuf2,
    send_sem, recv_sem, sel_sem, local_sem, gain_sem, q_ref, do_ref, in_sem,
):
    n, nx, nz, n_dp, chunks, heads, hd, block = (
        cfg[k] for k in ("n", "nx", "nz", "n_dp", "chunks", "heads", "hd", "block")
    )
    rows = block // n
    width = heads * hd // chunks
    per_chunk = heads // chunks
    scale = hd ** (-0.5)
    me = lax.axis_index("ctx")
    my_dp = lax.axis_index("dp")
    x, z = lax.div(me, nz), lax.rem(me, nz)
    up, down = lax.rem(me + 1, n), lax.rem(me + n - 1, n)

    def peer_of(kx, kz):
        return lax.rem(x + kx, nx) * nz + lax.rem(z + kz, nz)

    def each_peer(fn):
        def step(k, carry):
            fn(peer_of(lax.div(k, nz), lax.rem(k, nz)))
            return carry

        lax.fori_loop(1, n, step, 0)

    def each_z(fn):
        def step(k, carry):
            fn(peer_of(0, k), lax.rem(z + k, nz))
            return carry

        lax.fori_loop(1, nz, step, 0)

    def each_x(fn):
        for k in range(1, nx):
            fn(peer_of(k, 0), lax.rem(x + k, nx))

    def remote(src, dst, stage, c, peer):
        return pltpu.make_async_remote_copy(
            src_ref=src,
            dst_ref=dst,
            send_sem=send_sem.at[stage, c],
            recv_sem=recv_sem.at[stage, c],
            device_id={"ctx": peer},
            device_id_type=pl.DeviceIdType.MESH,
        )

    waits = []

    def landed(like, stage, c):
        remote(like, like, stage, c, up).wait_recv()
        waits.append((like, stage, c))

    HOLD, FETCH, BACK, COLL, PREV_F, PREV_B, AG_Z, AG_X, RS_X, RS_Z = range(10)

    load_q = pltpu.make_async_copy(q_hbm, q_ref, in_sem.at[0])
    load_do = pltpu.make_async_copy(do_hbm, do_ref, in_sem.at[1])
    load_q.start()
    load_do.start()
    barrier = pltpu.get_barrier_semaphore()

    def greet(peer):
        pl.semaphore_signal(
            barrier, inc=1, device_id={"ctx": peer}, device_id_type=pl.DeviceIdType.MESH
        )

    each_peer(greet)
    for k in range(1, n_dp):
        pl.semaphore_signal(
            barrier,
            inc=1,
            device_id={"dp": lax.rem(my_dp + k, n_dp)},
            device_id_type=pl.DeviceIdType.MESH,
        )

    def norm_chunk(c):
        def step(hh, carry):
            at = pl.ds(pl.multiple_of(hh * hd, hd), hd)
            wide = pl.ds(pl.multiple_of(c * width + hh * hd, hd), hd)
            xk = k_ref[0, :, wide].astype(F32)
            factor = lax.rsqrt(jnp.mean(xk * xk, axis=-1, keepdims=True) + EPS)
            kn = (xk * factor * kg_ref[...]).astype(BF16)
            kv[c, :, 0:rows, at] = kn.reshape(n, rows, hd)
            kv[c, :, rows : 2 * rows, at] = v_ref[0, :, wide].reshape(n, rows, hd)
            return carry

        lax.fori_loop(0, per_chunk, step, 0)

    gain_col = jnp.broadcast_to(qg_ref[...], (8, hd)).T[:, 0:1]
    norm_chunk(0)
    sub = lax.broadcasted_iota(jnp.int32, (8, 128), 0)
    lane = lax.broadcasted_iota(jnp.int32, (8, 128), 1)
    sel_tile[...] = jnp.where((sub < 4) | (lane == me), sel_ref[0, 0, 1], 0)
    pl.semaphore_wait(barrier, n - 1 + n_dp - 1)

    def send_table(peer):
        pltpu.make_async_remote_copy(
            src_ref=sel_tile,
            dst_ref=table.at[me],
            send_sem=sel_sem.at[0],
            recv_sem=sel_sem.at[1],
            device_id={"ctx": peer},
            device_id_type=pl.DeviceIdType.MESH,
        ).start()

    each_peer(send_table)
    table[me] = sel_tile[...]

    def send_hold(c):
        each_peer(lambda p: remote(kv.at[c, p], hold[c].at[me], HOLD, c, p).start())
        hold[c][me] = kv[c, me]

    def send_prev(c):
        remote(kv.at[c], prev.at[c], PREV_F, c, up).start()

    send_hold(0)
    for c in range(1, chunks):
        norm_chunk(c)

    some = pltpu.make_async_remote_copy(
        src_ref=table.at[pl.ds(0, n - 1)],
        dst_ref=table.at[pl.ds(0, n - 1)],
        send_sem=sel_sem.at[0],
        recv_sem=sel_sem.at[1],
        device_id={"ctx": up},
        device_id_type=pl.DeviceIdType.MESH,
    )
    some.wait_recv()
    choice = table[:, 0, :]
    spread_out = table[0, 4:8, :]
    for i in range(1, n):
        spread_out = spread_out + table[i, 4:8, :]
    across = jnp.broadcast_to(spread_out[0:1, :], (n, 128))
    row_id = lax.broadcasted_iota(jnp.int32, (n, 128), 0)
    lane_id = lax.broadcasted_iota(jnp.int32, (n, 128), 1)
    before = jnp.where((across == choice) & (lane_id < row_id), lane_id, -1)
    last = jnp.where((across == row_id) & (lane_id < n), lane_id, -1)
    links_v[0] = choice
    for k, found in ((1, before), (2, last)):
        top = jnp.max(found, axis=-1, keepdims=True)
        links_v[k] = jnp.broadcast_to(jnp.where(top < 0, n, top), (n, 128))
    to_scalars = pltpu.make_async_copy(links_v, links, local_sem)
    to_scalars.start()
    to_scalars.wait()

    def link(kind, i):
        return jnp.clip(links[kind, i, 0], 0, n if kind else n - 1)

    def serve(c):
        landed(hold[c].at[pl.ds(0, n - 1)], HOLD, c)
        first[c, me] = hold[c][0]
        each_z(lambda p, _: remote(first.at[c, me], first.at[c, me], AG_Z, c, p).start())

        def send(p):
            pick[c, p] = hold[c][link(0, p)]
            remote(pick.at[c, p], fetch.at[c, me], FETCH, c, p).start()

        each_peer(send)
        fetch[c, me] = hold[c][link(0, me)]

    def spread(c):
        landed(first.at[c, pl.ds(0, nz - 1)], AG_Z, c)
        row = pl.ds(x * nz, nz)
        each_x(lambda p, _: remote(first.at[c, row], first.at[c, row], AG_X, c, p).start())

    def prepare(c):
        serve(c)
        if c + 1 < chunks:
            send_hold(c + 1)
        send_prev(c)
        spread(c)

    prepare(0)
    load_q.wait()
    load_do.wait()

    see_prev = (me >= 2).astype(F32)
    see_first = (me >= 1).astype(F32)
    see_mid = jnp.where(links[0, me, 0] != me, 1.0, 0.0).astype(F32)
    see = (None, see_prev, see_first, see_mid)
    stores = (kv, prev, first, fetch)

    def seen(value, b):
        return value if see[b] is None else value * see[b]

    gq[...] = jnp.zeros_like(gq)
    gk[...] = jnp.zeros_like(gk)

    def attend(c):
        def step(hh, carry):
            at = pl.ds(pl.multiple_of(hh * hd, hd), hd)
            wide = pl.ds(pl.multiple_of(c * width + hh * hd, hd), hd)
            xt = q_ref[0, :, wide].astype(F32).T
            factor = lax.rsqrt(jnp.mean(xt * xt, axis=0, keepdims=True) + EPS)
            gain = gain_col
            qn = (xt * factor * gain).astype(BF16)
            do = do_ref[0, :, wide].astype(F32).T
            do_b = do.astype(BF16)

            def keys(b):
                return stores[b][c, :, 0:rows, at].reshape(block, hd)

            def values(b):
                return stores[b][c, :, rows : 2 * rows, at].reshape(block, hd)

            total = jnp.zeros((1, block), F32)
            acc = jnp.zeros((hd, block), F32)
            for b in (OWN, PREV, FIRST, MID):
                s = dot(keys(b), qn, ((1,), (0,)))
                w = jnp.exp2(s * (scale * 1.4426950408889634))
                if b == OWN:
                    ki = lax.broadcasted_iota(jnp.int32, (block, block), 0)
                    qi = lax.broadcasted_iota(jnp.int32, (block, block), 1)
                    w = jnp.where(ki <= qi, w, 0.0)
                total = total + seen(jnp.sum(w, axis=0, keepdims=True), b)
                wb = w.astype(BF16)
                w_scr[b] = wb
                acc = acc + seen(dot(values(b), wb, ((0,), (0,))), b)
            inv = 1.0 / total
            out = (acc * inv).astype(BF16).astype(F32)
            att_ref[0, :, wide] = out.T.astype(BF16)
            delta = jnp.sum(do * out, axis=0, keepdims=True)
            inv_s = inv * scale
            qs = (qn.astype(F32) * inv_s).astype(BF16)
            dos = (do * inv).astype(BF16)
            dq = jnp.zeros((hd, block), F32)
            for b in (MID, FIRST, PREV, OWN):
                wb = w_scr[b]
                dp = dot(values(b), do_b, ((1,), (0,)))
                ds = (wb.astype(F32) * (dp - delta)).astype(BF16)
                dq = dq + seen(dot(keys(b), ds, ((0,), (0,))), b)
                dk = seen(dot(ds, qs, ((1,), (1,))), b)
                dv = seen(dot(wb, dos, ((1,), (1,))), b)
                if b == OWN:
                    own_grad[0, :, wide] = dk
                    own_grad[1, :, wide] = dv
                else:
                    term[b - 1, c, :, 0:rows, at] = dk.astype(BF16).reshape(n, rows, hd)
                    term[b - 1, c, :, rows : 2 * rows, at] = dv.astype(BF16).reshape(n, rows, hd)
            dy = dq * inv_s
            xr = xt * factor
            both = dy * xr
            g = both[:, 0:hd]
            for k in range(1, block // hd):
                g = g + both[:, k * hd : (k + 1) * hd]
            gq[...] += g
            u = dy * gain
            dx = factor * (u - xr * jnp.mean(xr * u, axis=0, keepdims=True))
            dq_ref[0, :, wide] = dx.T.astype(BF16)
            return carry

        lax.fori_loop(0, per_chunk, step, 0)

    def give_back(c):
        mid, head = term.at[MID - 1, c], term.at[FIRST - 1, c]
        each_peer(lambda p: remote(mid.at[p], back.at[c, me], BACK, c, p).start())
        back[c, me] = term[MID - 1, c, me]

        def send_row(p, px):
            remote(head.at[pl.ds(px * nz, nz)], rx.at[c, x], RS_X, c, p).start()

        each_x(send_row)
        rx[c, x] = term[FIRST - 1, c, pl.ds(x * nz, nz)]
        if c + 1 < chunks:
            send_prev_back(c)

    def send_prev_back(c):
        remote(term.at[PREV - 1, c], prev_back.at[c], PREV_B, c, down).start()

    def fold_first(c):
        landed(rx.at[c, pl.ds(0, nx - 1)], RS_X, c)

        def fold(s, carry):
            total = rx[c, 0, s].astype(F32)
            for k in range(1, nx):
                total = total + rx[c, k, s].astype(F32)
            rz_out[c, s] = total.astype(BF16)
            return carry

        lax.fori_loop(0, nz, fold, 0)
        each_z(lambda p, pz: remote(rz_out.at[c, pz], rz.at[c, z], RS_Z, c, p).start())
        rz[c, z] = rz_out[c, z]

    def collect(c):
        landed(back.at[c, pl.ds(0, n - 1)], BACK, c)
        if c + 1 == chunks:
            send_prev_back(c)
        part[n] = jnp.zeros(part.shape[1:], F32)

        def add(i, carry):
            part[i] = back[c, i].astype(F32) + part[link(1, i)]
            return carry

        lax.fori_loop(0, n, add, 0)

        def settle(j, carry):
            sums[c, j] = part[link(2, j)].astype(BF16)
            return carry

        lax.fori_loop(1, n, settle, 0)
        landed(rz.at[c, pl.ds(0, nz - 1)], RS_Z, c)
        total = part[link(2, 0)]
        for k in range(nz):
            total = total + rz[c, k].astype(F32)
        sums[c, 0] = total.astype(BF16)
        each_peer(lambda p: remote(sums.at[c, p], coll.at[c, me], COLL, c, p).start())
        coll[c, me] = sums[c, me]

    def finish(c):
        landed(prev_back.at[c], PREV_B, c)
        landed(coll.at[c, pl.ds(0, n - 1)], COLL, c)

        def step(hh, carry):
            at = pl.ds(pl.multiple_of(hh * hd, hd), hd)
            wide = pl.ds(pl.multiple_of(c * width + hh * hd, hd), hd)

            def remote_sum(lo):
                one = coll[c, :, lo : lo + rows, at].reshape(block, hd).astype(F32)
                two = prev_back[c, :, lo : lo + rows, at].reshape(block, hd).astype(F32)
                return one + two

            dv_ref[0, :, wide] = (own_grad[1, :, wide] + remote_sum(rows)).astype(BF16)
            dy = own_grad[0, :, wide] + remote_sum(0)
            xk = k_ref[0, :, wide].astype(F32)
            factor = lax.rsqrt(jnp.mean(xk * xk, axis=-1, keepdims=True) + EPS)
            xr = xk * factor
            gk[...] += jnp.sum((dy * xr).reshape(block // 8, 8, hd), axis=0)
            u = dy * kg_ref[...]
            dx = factor * (u - xr * jnp.mean(xr * u, axis=-1, keepdims=True))
            dk_ref[0, :, wide] = dx.astype(BF16)
            return carry

        lax.fori_loop(0, per_chunk, step, 0)

    for c in range(chunks):
        if c + 1 < chunks:
            prepare(c + 1)
        landed(prev.at[c], PREV_F, c)
        landed(fetch.at[c, pl.ds(0, n - 1)], FETCH, c)
        landed(first.at[c, pl.ds(0, (nx - 1) * nz)], AG_X, c)
        attend(c)
        give_back(c)
        if c >= 1:
            fold_first(c - 1)
            collect(c - 1)
    fold_first(chunks - 1)
    collect(chunks - 1)
    for c in range(chunks):
        finish(c)

    q_row = jnp.sum(gq[...].T, axis=0, keepdims=True)
    k_row = jnp.sum(gk[...], axis=0, keepdims=True)
    at = lax.broadcasted_iota(jnp.int32, (8, hd), 0)
    gbuf[me] = jnp.where(at == 0, q_row, jnp.where(at == 1, k_row, 0.0))

    def send_gain(buf, slot, at, where):
        return pltpu.make_async_remote_copy(
            src_ref=buf.at[slot],
            dst_ref=buf.at[slot],
            send_sem=gain_sem.at[at, 0],
            recv_sem=gain_sem.at[at, 1],
            device_id=where,
            device_id_type=pl.DeviceIdType.MESH,
        )

    def all_gain(buf, count, at):
        many = buf.at[pl.ds(0, count - 1)]
        return pltpu.make_async_remote_copy(
            src_ref=many,
            dst_ref=many,
            send_sem=gain_sem.at[at, 0],
            recv_sem=gain_sem.at[at, 1],
            device_id={"ctx": up},
            device_id_type=pl.DeviceIdType.MESH,
        )

    each_peer(lambda p: send_gain(gbuf, me, 0, {"ctx": p}).start())
    all_gain(gbuf, n, 0).wait_recv()
    total = gbuf[0]
    for i in range(1, n):
        total = total + gbuf[i]
    gbuf2[my_dp] = total
    for k in range(1, n_dp):
        send_gain(gbuf2, my_dp, 1, {"dp": lax.rem(my_dp + k, n_dp)}).start()
    all_gain(gbuf2, n_dp, 1).wait_recv()
    total = gbuf2[0]
    for i in range(1, n_dp):
        total = total + gbuf2[i]
    q_gain_ref[...] = total[0:1, :]
    k_gain_ref[...] = total[1:2, :]

    all_gain(gbuf, n, 0).wait_send()
    all_gain(gbuf2, n_dp, 1).wait_send()
    some.wait_send()
    for like, stage, c in waits:
        remote(like, like, stage, c, up).wait_send()


def hand_over(*refs):
    for given, taken in zip(refs[0:6], refs[6:12], strict=True):
        taken[...] = given[...]


def local(mesh_shape, query_rows, key_rows, value_rows, query_gain, key_gain, selected, output_grad):
    n, n_dp = mesh_shape["ctx"], mesh_shape["dp"]
    nz = 8 if n == 32 else n // 2
    nx = n // nz
    block, model = query_rows.shape[1:]
    hd = query_gain.shape[0]
    heads = model // hd
    chunks = CHUNKS
    cfg = dict(n=n, nx=nx, nz=nz, n_dp=n_dp, chunks=chunks, heads=heads, hd=hd, block=block)
    width, rows = model // chunks, block // n
    slices = (chunks, n, 2 * rows, width)
    vmem = pltpu.VMEM
    row = jax.ShapeDtypeStruct((1, block, model), BF16)
    gain = jax.ShapeDtypeStruct((1, hd), F32)
    whole = pl.BlockSpec(memory_space=pltpu.VMEM)
    anywhere = pl.BlockSpec(memory_space=pl.ANY)
    outs = pl.pallas_call(
        functools.partial(body, cfg),
        out_shape=(row, row, row, row, gain, gain),
        in_specs=[anywhere] + [whole] * 4 + [pl.BlockSpec(memory_space=pltpu.SMEM), anywhere],
        out_specs=(whole,) * 6,
        scratch_shapes=[
            vmem(slices, BF16),
            [vmem(slices[1:], BF16)] * chunks,
            vmem(slices, BF16),
            vmem(slices, BF16),
            vmem(slices, BF16),
            vmem(slices, BF16),
            vmem((4, block, block), BF16),
            vmem((3,) + slices, BF16),
            vmem((2, block, model), F32),
            vmem(slices, BF16),
            vmem((n + 1, 2 * rows, width), F32),
            vmem(slices, BF16),
            vmem(slices, BF16),
            vmem(slices, BF16),
            vmem((chunks, nx, nz, 2 * rows, width), BF16),
            vmem((chunks, nz, 2 * rows, width), BF16),
            vmem((chunks, nz, 2 * rows, width), BF16),
            vmem((8, 128), jnp.int32),
            vmem((n, 8, 128), jnp.int32),
            vmem((3, n, 128), jnp.int32),
            pltpu.SMEM((3, n, 128), jnp.int32),
            vmem((hd, hd), F32),
            vmem((8, hd), F32),
            vmem((n, 8, hd), F32),
            vmem((n_dp, 8, hd), F32),
            pltpu.SemaphoreType.DMA((10, chunks)),
            pltpu.SemaphoreType.DMA((10, chunks)),
            pltpu.SemaphoreType.DMA((2,)),
            pltpu.SemaphoreType.DMA,
            pltpu.SemaphoreType.DMA((2, 2)),
            vmem((1, block, model), BF16),
            vmem((1, block, model), BF16),
            pltpu.SemaphoreType.DMA((2,)),
        ],
        compiler_params=pltpu.CompilerParams(
            collective_id=0, has_side_effects=True, vmem_limit_bytes=60 * 1024 * 1024
        ),
    )(
        query_rows,
        key_rows,
        value_rows,
        query_gain.reshape(1, hd),
        key_gain.reshape(1, hd),
        selected,
        output_grad,
    )
    steps = 4
    part = pl.BlockSpec((1, block // steps, model), lambda i: (0, i, 0))
    line = pl.BlockSpec((1, hd), lambda i: (0, 0))
    outs = pl.pallas_call(
        hand_over,
        out_shape=(row, row, row, row, gain, gain),
        grid=(steps,),
        in_specs=[part] * 4 + [line] * 2,
        out_specs=(part,) * 4 + (line,) * 2,
    )(*outs)
    attended, query_grad, key_grad, value_grad, q_gain, k_gain = outs
    return attended, query_grad, key_grad, value_grad, q_gain.reshape(hd), k_gain.reshape(hd)


def solution(mesh):
    rows = P("dp", "ctx", None)
    return jax.shard_map(
        functools.partial(local, dict(mesh.shape)),
        mesh=mesh,
        in_specs=(rows, rows, rows, P(), P(), rows, rows),
        out_specs=(rows, rows, rows, rows, P(), P()),
        check_vma=False,
    )
```

```python
import functools

import jax
import jax.numpy as jnp
from jax import lax
from jax.experimental import pallas as pl
from jax.experimental.pallas import tpu as pltpu
from jax.sharding import PartitionSpec as P

CHUNKS = 4
EPS = 1e-06
OWN, PREV, FIRST, MID = 0, 1, 2, 3
F32, BF16 = jnp.float32, jnp.bfloat16


def dot(left, right, dims):
    return lax.dot_general(left, right, (dims, ((), ())), preferred_element_type=F32)


def body(
    cfg,
    q_hbm, k_ref, v_ref, qg_ref, kg_ref, sel_ref, do_hbm,
    att_ref, dq_ref, dk_ref, dv_ref, q_gain_ref, k_gain_ref,
    kv, hold, pick, fetch, prev, first, w_scr,
    term, own_grad, back, part, sums, coll, prev_back, rx, rz_out, rz,
    sel_tile, table, links_v, links, gq, gk, gbuf, gbuf2,
    send_sem, recv_sem, sel_sem, local_sem, gain_sem, q_ref, do_ref, in_sem,
):
    n, nx, nz, n_dp, chunks, heads, hd, block = (
        cfg[k] for k in ("n", "nx", "nz", "n_dp", "chunks", "heads", "hd", "block")
    )
    rows = block // n
    width = heads * hd // chunks
    per_chunk = heads // chunks
    scale = hd ** (-0.5)
    me = lax.axis_index("ctx")
    my_dp = lax.axis_index("dp")
    x, z = lax.div(me, nz), lax.rem(me, nz)
    up, down = lax.rem(me + 1, n), lax.rem(me + n - 1, n)

    def peer_of(kx, kz):
        return lax.rem(x + kx, nx) * nz + lax.rem(z + kz, nz)

    def each_peer(fn):
        def step(k, carry):
            fn(peer_of(lax.div(k, nz), lax.rem(k, nz)))
            return carry

        lax.fori_loop(1, n, step, 0)

    def each_z(fn):
        def step(k, carry):
            fn(peer_of(0, k), lax.rem(z + k, nz))
            return carry

        lax.fori_loop(1, nz, step, 0)

    def each_x(fn):
        for k in range(1, nx):
            fn(peer_of(k, 0), lax.rem(x + k, nx))

    def remote(src, dst, stage, c, peer):
        return pltpu.make_async_remote_copy(
            src_ref=src,
            dst_ref=dst,
            send_sem=send_sem.at[stage, c],
            recv_sem=recv_sem.at[stage, c],
            device_id={"ctx": peer},
            device_id_type=pl.DeviceIdType.MESH,
        )

    waits = []

    def landed(like, stage, c):
        remote(like, like, stage, c, up).wait_recv()
        waits.append((like, stage, c))

    HOLD, FETCH, BACK, COLL, PREV_F, PREV_B, AG_Z, AG_X, RS_X, RS_Z = range(10)

    load_q = pltpu.make_async_copy(q_hbm, q_ref, in_sem.at[0])
    load_do = pltpu.make_async_copy(do_hbm, do_ref, in_sem.at[1])
    load_q.start()
    load_do.start()
    barrier = pltpu.get_barrier_semaphore()

    def greet(peer):
        pl.semaphore_signal(
            barrier, inc=1, device_id={"ctx": peer}, device_id_type=pl.DeviceIdType.MESH
        )

    each_peer(greet)
    for k in range(1, n_dp):
        pl.semaphore_signal(
            barrier,
            inc=1,
            device_id={"dp": lax.rem(my_dp + k, n_dp)},
            device_id_type=pl.DeviceIdType.MESH,
        )

    def norm_chunk(c):
        def step(hh, carry):
            at = pl.ds(pl.multiple_of(hh * hd, hd), hd)
            wide = pl.ds(pl.multiple_of(c * width + hh * hd, hd), hd)
            xk = k_ref[0, :, wide].astype(F32)
            factor = lax.rsqrt(jnp.mean(xk * xk, axis=-1, keepdims=True) + EPS)
            kn = (xk * factor * kg_ref[...]).astype(BF16)
            kv[c, :, 0:rows, at] = kn.reshape(n, rows, hd)
            kv[c, :, rows : 2 * rows, at] = v_ref[0, :, wide].reshape(n, rows, hd)
            return carry

        lax.fori_loop(0, per_chunk, step, 0)

    gain_col = jnp.broadcast_to(qg_ref[...], (8, hd)).T[:, 0:1]
    norm_chunk(0)
    sub = lax.broadcasted_iota(jnp.int32, (8, 128), 0)
    lane = lax.broadcasted_iota(jnp.int32, (8, 128), 1)
    sel_tile[...] = jnp.where((sub < 4) | (lane == me), sel_ref[0, 0, 1], 0)
    pl.semaphore_wait(barrier, n - 1 + n_dp - 1)

    def send_table(peer):
        pltpu.make_async_remote_copy(
            src_ref=sel_tile,
            dst_ref=table.at[me],
            send_sem=sel_sem.at[0],
            recv_sem=sel_sem.at[1],
            device_id={"ctx": peer},
            device_id_type=pl.DeviceIdType.MESH,
        ).start()

    each_peer(send_table)
    table[me] = sel_tile[...]

    def send_hold(c):
        each_peer(lambda p: remote(kv.at[c, p], hold[c].at[me], HOLD, c, p).start())
        hold[c][me] = kv[c, me]

    def send_prev(c):
        remote(kv.at[c], prev.at[c], PREV_F, c, up).start()

    send_hold(0)
    for c in range(1, chunks):
        norm_chunk(c)

    some = pltpu.make_async_remote_copy(
        src_ref=table.at[pl.ds(0, n - 1)],
        dst_ref=table.at[pl.ds(0, n - 1)],
        send_sem=sel_sem.at[0],
        recv_sem=sel_sem.at[1],
        device_id={"ctx": up},
        device_id_type=pl.DeviceIdType.MESH,
    )
    some.wait_recv()
    choice = table[:, 0, :]
    spread_out = table[0, 4:8, :]
    for i in range(1, n):
        spread_out = spread_out + table[i, 4:8, :]
    across = jnp.broadcast_to(spread_out[0:1, :], (n, 128))
    row_id = lax.broadcasted_iota(jnp.int32, (n, 128), 0)
    lane_id = lax.broadcasted_iota(jnp.int32, (n, 128), 1)
    before = jnp.where((across == choice) & (lane_id < row_id), lane_id, -1)
    last = jnp.where((across == row_id) & (lane_id < n), lane_id, -1)
    links_v[0] = choice
    for k, found in ((1, before), (2, last)):
        top = jnp.max(found, axis=-1, keepdims=True)
        links_v[k] = jnp.broadcast_to(jnp.where(top < 0, n, top), (n, 128))
    to_scalars = pltpu.make_async_copy(links_v, links, local_sem)
    to_scalars.start()
    to_scalars.wait()

    def link(kind, i):
        return jnp.clip(links[kind, i, 0], 0, n if kind else n - 1)

    def serve(c):
        landed(hold[c].at[pl.ds(0, n - 1)], HOLD, c)
        first[c, me] = hold[c][0]
        each_z(lambda p, _: remote(first.at[c, me], first.at[c, me], AG_Z, c, p).start())

        def send(p):
            pick[c, p] = hold[c][link(0, p)]
            remote(pick.at[c, p], fetch.at[c, me], FETCH, c, p).start()

        each_peer(send)
        fetch[c, me] = hold[c][link(0, me)]

    def spread(c):
        landed(first.at[c, pl.ds(0, nz - 1)], AG_Z, c)
        row = pl.ds(x * nz, nz)
        each_x(lambda p, _: remote(first.at[c, row], first.at[c, row], AG_X, c, p).start())

    def prepare(c):
        serve(c)
        if c + 1 < chunks:
            send_hold(c + 1)
        send_prev(c)
        spread(c)

    prepare(0)
    load_q.wait()
    load_do.wait()

    see_prev = (me >= 2).astype(F32)
    see_first = (me >= 1).astype(F32)
    see_mid = jnp.where(links[0, me, 0] != me, 1.0, 0.0).astype(F32)
    see = (None, see_prev, see_first, see_mid)
    stores = (kv, prev, first, fetch)

    def seen(value, b):
        return value if see[b] is None else value * see[b]

    gq[...] = jnp.zeros_like(gq)
    gk[...] = jnp.zeros_like(gk)

    def attend(c):
        def step(hh, carry):
            at = pl.ds(pl.multiple_of(hh * hd, hd), hd)
            wide = pl.ds(pl.multiple_of(c * width + hh * hd, hd), hd)
            xt = q_ref[0, :, wide].astype(F32).T
            factor = lax.rsqrt(jnp.mean(xt * xt, axis=0, keepdims=True) + EPS)
            gain = gain_col
            qn = (xt * factor * gain).astype(BF16)
            do = do_ref[0, :, wide].astype(F32).T
            do_b = do.astype(BF16)

            def keys(b):
                return stores[b][c, :, 0:rows, at].reshape(block, hd)

            def values(b):
                return stores[b][c, :, rows : 2 * rows, at].reshape(block, hd)

            total = jnp.zeros((1, block), F32)
            acc = jnp.zeros((hd, block), F32)
            for b in (OWN, PREV, FIRST, MID):
                s = dot(keys(b), qn, ((1,), (0,)))
                w = jnp.exp2(s * (scale * 1.4426950408889634))
                if b == OWN:
                    ki = lax.broadcasted_iota(jnp.int32, (block, block), 0)
                    qi = lax.broadcasted_iota(jnp.int32, (block, block), 1)
                    w = jnp.where(ki <= qi, w, 0.0)
                total = total + seen(jnp.sum(w, axis=0, keepdims=True), b)
                wb = w.astype(BF16)
                w_scr[b] = wb
                acc = acc + seen(dot(values(b), wb, ((0,), (0,))), b)
            inv = 1.0 / total
            out = (acc * inv).astype(BF16).astype(F32)
            att_ref[0, :, wide] = out.T.astype(BF16)
            delta = jnp.sum(do * out, axis=0, keepdims=True)
            inv_s = inv * scale
            qs = (qn.astype(F32) * inv_s).astype(BF16)
            dos = (do * inv).astype(BF16)
            dq = jnp.zeros((hd, block), F32)
            for b in (MID, FIRST, PREV, OWN):
                wb = w_scr[b]
                dp = dot(values(b), do_b, ((1,), (0,)))
                ds = (wb.astype(F32) * (dp - delta)).astype(BF16)
                dq = dq + seen(dot(keys(b), ds, ((0,), (0,))), b)
                dk = seen(dot(ds, qs, ((1,), (1,))), b)
                dv = seen(dot(wb, dos, ((1,), (1,))), b)
                if b == OWN:
                    own_grad[0, :, wide] = dk
                    own_grad[1, :, wide] = dv
                else:
                    term[b - 1, c, :, 0:rows, at] = dk.astype(BF16).reshape(n, rows, hd)
                    term[b - 1, c, :, rows : 2 * rows, at] = dv.astype(BF16).reshape(n, rows, hd)
            dy = dq * inv_s
            xr = xt * factor
            both = dy * xr
            g = both[:, 0:hd]
            for k in range(1, block // hd):
                g = g + both[:, k * hd : (k + 1) * hd]
            gq[...] += g
            u = dy * gain
            dx = factor * (u - xr * jnp.mean(xr * u, axis=0, keepdims=True))
            dq_ref[0, :, wide] = dx.T.astype(BF16)
            return carry

        lax.fori_loop(0, per_chunk, step, 0)

    def give_back(c):
        mid, head = term.at[MID - 1, c], term.at[FIRST - 1, c]
        each_peer(lambda p: remote(mid.at[p], back.at[c, me], BACK, c, p).start())
        back[c, me] = term[MID - 1, c, me]

        def send_row(p, px):
            remote(head.at[pl.ds(px * nz, nz)], rx.at[c, x], RS_X, c, p).start()

        each_x(send_row)
        rx[c, x] = term[FIRST - 1, c, pl.ds(x * nz, nz)]
        if c + 1 < chunks:
            send_prev_back(c)

    def send_prev_back(c):
        remote(term.at[PREV - 1, c], prev_back.at[c], PREV_B, c, down).start()

    def fold_first(c):
        landed(rx.at[c, pl.ds(0, nx - 1)], RS_X, c)

        def fold(s, carry):
            total = rx[c, 0, s].astype(F32)
            for k in range(1, nx):
                total = total + rx[c, k, s].astype(F32)
            rz_out[c, s] = total.astype(BF16)
            return carry

        lax.fori_loop(0, nz, fold, 0)
        each_z(lambda p, pz: remote(rz_out.at[c, pz], rz.at[c, z], RS_Z, c, p).start())
        rz[c, z] = rz_out[c, z]

    def collect(c):
        landed(back.at[c, pl.ds(0, n - 1)], BACK, c)
        if c + 1 == chunks:
            send_prev_back(c)
        part[n] = jnp.zeros(part.shape[1:], F32)

        def add(i, carry):
            part[i] = back[c, i].astype(F32) + part[link(1, i)]
            return carry

        lax.fori_loop(0, n, add, 0)

        def settle(j, carry):
            sums[c, j] = part[link(2, j)].astype(BF16)
            return carry

        lax.fori_loop(1, n, settle, 0)

        def settled(p):
            @pl.when(p != 0)
            def _():
                remote(sums.at[c, p], coll.at[c, me], COLL, c, p).start()

        each_peer(settled)
        landed(rz.at[c, pl.ds(0, nz - 1)], RS_Z, c)
        total = part[link(2, 0)]
        for k in range(nz):
            total = total + rz[c, k].astype(F32)
        sums[c, 0] = total.astype(BF16)

        @pl.when(me != 0)
        def _():
            remote(sums.at[c, 0], coll.at[c, me], COLL, c, 0).start()

        coll[c, me] = sums[c, me]

    def finish(c):
        landed(prev_back.at[c], PREV_B, c)
        landed(coll.at[c, pl.ds(0, n - 1)], COLL, c)

        def step(hh, carry):
            at = pl.ds(pl.multiple_of(hh * hd, hd), hd)
            wide = pl.ds(pl.multiple_of(c * width + hh * hd, hd), hd)

            def remote_sum(lo):
                one = coll[c, :, lo : lo + rows, at].reshape(block, hd).astype(F32)
                two = prev_back[c, :, lo : lo + rows, at].reshape(block, hd).astype(F32)
                return one + two

            dv_ref[0, :, wide] = (own_grad[1, :, wide] + remote_sum(rows)).astype(BF16)
            dy = own_grad[0, :, wide] + remote_sum(0)
            xk = k_ref[0, :, wide].astype(F32)
            factor = lax.rsqrt(jnp.mean(xk * xk, axis=-1, keepdims=True) + EPS)
            xr = xk * factor
            gk[...] += jnp.sum((dy * xr).reshape(block // 8, 8, hd), axis=0)
            u = dy * kg_ref[...]
            dx = factor * (u - xr * jnp.mean(xr * u, axis=-1, keepdims=True))
            dk_ref[0, :, wide] = dx.astype(BF16)
            return carry

        lax.fori_loop(0, per_chunk, step, 0)

    for c in range(chunks):
        if c + 1 < chunks:
            prepare(c + 1)
        landed(prev.at[c], PREV_F, c)
        landed(fetch.at[c, pl.ds(0, n - 1)], FETCH, c)
        landed(first.at[c, pl.ds(0, (nx - 1) * nz)], AG_X, c)
        attend(c)
        give_back(c)
        if c >= 1:
            fold_first(c - 1)
            collect(c - 1)
    fold_first(chunks - 1)
    collect(chunks - 1)
    for c in range(chunks):
        finish(c)

    q_row = jnp.sum(gq[...].T, axis=0, keepdims=True)
    k_row = jnp.sum(gk[...], axis=0, keepdims=True)
    at = lax.broadcasted_iota(jnp.int32, (8, hd), 0)
    gbuf[me] = jnp.where(at == 0, q_row, jnp.where(at == 1, k_row, 0.0))

    def send_gain(buf, slot, at, where):
        return pltpu.make_async_remote_copy(
            src_ref=buf.at[slot],
            dst_ref=buf.at[slot],
            send_sem=gain_sem.at[at, 0],
            recv_sem=gain_sem.at[at, 1],
            device_id=where,
            device_id_type=pl.DeviceIdType.MESH,
        )

    def all_gain(buf, count, at):
        many = buf.at[pl.ds(0, count - 1)]
        return pltpu.make_async_remote_copy(
            src_ref=many,
            dst_ref=many,
            send_sem=gain_sem.at[at, 0],
            recv_sem=gain_sem.at[at, 1],
            device_id={"ctx": up},
            device_id_type=pl.DeviceIdType.MESH,
        )

    each_peer(lambda p: send_gain(gbuf, me, 0, {"ctx": p}).start())
    all_gain(gbuf, n, 0).wait_recv()
    total = gbuf[0]
    for i in range(1, n):
        total = total + gbuf[i]
    gbuf2[my_dp] = total
    for k in range(1, n_dp):
        send_gain(gbuf2, my_dp, 1, {"dp": lax.rem(my_dp + k, n_dp)}).start()
    all_gain(gbuf2, n_dp, 1).wait_recv()
    total = gbuf2[0]
    for i in range(1, n_dp):
        total = total + gbuf2[i]
    q_gain_ref[...] = total[0:1, :]
    k_gain_ref[...] = total[1:2, :]

    all_gain(gbuf, n, 0).wait_send()
    all_gain(gbuf2, n_dp, 1).wait_send()
    some.wait_send()
    for like, stage, c in waits:
        remote(like, like, stage, c, up).wait_send()


def hand_over(*refs):
    for given, taken in zip(refs[0:6], refs[6:12], strict=True):
        taken[...] = given[...]


def local(mesh_shape, query_rows, key_rows, value_rows, query_gain, key_gain, selected, output_grad):
    n, n_dp = mesh_shape["ctx"], mesh_shape["dp"]
    nz = 8 if n == 32 else n // 2
    nx = n // nz
    block, model = query_rows.shape[1:]
    hd = query_gain.shape[0]
    heads = model // hd
    chunks = CHUNKS
    cfg = dict(n=n, nx=nx, nz=nz, n_dp=n_dp, chunks=chunks, heads=heads, hd=hd, block=block)
    width, rows = model // chunks, block // n
    slices = (chunks, n, 2 * rows, width)
    vmem = pltpu.VMEM
    row = jax.ShapeDtypeStruct((1, block, model), BF16)
    gain = jax.ShapeDtypeStruct((1, hd), F32)
    whole = pl.BlockSpec(memory_space=pltpu.VMEM)
    anywhere = pl.BlockSpec(memory_space=pl.ANY)
    outs = pl.pallas_call(
        functools.partial(body, cfg),
        out_shape=(row, row, row, row, gain, gain),
        in_specs=[anywhere] + [whole] * 4 + [pl.BlockSpec(memory_space=pltpu.SMEM), anywhere],
        out_specs=(whole,) * 6,
        scratch_shapes=[
            vmem(slices, BF16),
            [vmem(slices[1:], BF16)] * chunks,
            vmem(slices, BF16),
            vmem(slices, BF16),
            vmem(slices, BF16),
            vmem(slices, BF16),
            vmem((4, block, block), BF16),
            vmem((3,) + slices, BF16),
            vmem((2, block, model), F32),
            vmem(slices, BF16),
            vmem((n + 1, 2 * rows, width), F32),
            vmem(slices, BF16),
            vmem(slices, BF16),
            vmem(slices, BF16),
            vmem((chunks, nx, nz, 2 * rows, width), BF16),
            vmem((chunks, nz, 2 * rows, width), BF16),
            vmem((chunks, nz, 2 * rows, width), BF16),
            vmem((8, 128), jnp.int32),
            vmem((n, 8, 128), jnp.int32),
            vmem((3, n, 128), jnp.int32),
            pltpu.SMEM((3, n, 128), jnp.int32),
            vmem((hd, hd), F32),
            vmem((8, hd), F32),
            vmem((n, 8, hd), F32),
            vmem((n_dp, 8, hd), F32),
            pltpu.SemaphoreType.DMA((10, chunks)),
            pltpu.SemaphoreType.DMA((10, chunks)),
            pltpu.SemaphoreType.DMA((2,)),
            pltpu.SemaphoreType.DMA,
            pltpu.SemaphoreType.DMA((2, 2)),
            vmem((1, block, model), BF16),
            vmem((1, block, model), BF16),
            pltpu.SemaphoreType.DMA((2,)),
        ],
        compiler_params=pltpu.CompilerParams(
            collective_id=0, has_side_effects=True, vmem_limit_bytes=60 * 1024 * 1024
        ),
    )(
        query_rows,
        key_rows,
        value_rows,
        query_gain.reshape(1, hd),
        key_gain.reshape(1, hd),
        selected,
        output_grad,
    )
    steps = 4
    part = pl.BlockSpec((1, block // steps, model), lambda i: (0, i, 0))
    line = pl.BlockSpec((1, hd), lambda i: (0, 0))
    outs = pl.pallas_call(
        hand_over,
        out_shape=(row, row, row, row, gain, gain),
        grid=(steps,),
        in_specs=[part] * 4 + [line] * 2,
        out_specs=(part,) * 4 + (line,) * 2,
    )(*outs)
    attended, query_grad, key_grad, value_grad, q_gain, k_gain = outs
    return attended, query_grad, key_grad, value_grad, q_gain.reshape(hd), k_gain.reshape(hd)


def solution(mesh):
    rows = P("dp", "ctx", None)
    return jax.shard_map(
        functools.partial(local, dict(mesh.shape)),
        mesh=mesh,
        in_specs=(rows, rows, rows, P(), P(), rows, rows),
        out_specs=(rows, rows, rows, rows, P(), P()),
        check_vma=False,
    )
```
